32 devices in a mesh: row: 4 (over z), col: 8 (over y, x, core).
Axes of the slice: x: 2, y: 2, z: 4, core: 2. Of those that a mesh axis runs over, the one named last changes fastest.
Arguments:
- tokens: bfloat16 [2048, 8192], P('row', 'col'), may hold values from -6 to 6
- weight: bfloat16 [8192, 26624], P('row', 'col'), may hold values from -0.0625 to 0.0625
- out_grad: bfloat16 [2048, 26624], P('row', 'col'), may hold values from -6 to 6
Outputs:
- preact: bfloat16 [2048, 26624], P('row', 'col')
- input_grad: bfloat16 [2048, 8192], P('row', 'col')
The draws below stay inside these ranges and needn't reach their ends.
All inputs are finite; a program needn't handle non-finite values.
Results may differ from the reference program's by a relative error of at most 0.0049.
Values may be sent and summed in bfloat16 or wider, within the bound.
A program may use at most 192 MiB of HBM per device.

```python
import math
import jax
import jax.numpy as jnp

D = 8192
FF = 26624
TOKENS = 2048


def block_scale(rng, dims, shards, low, largest):
    gain = 1.0
    for dim, blocks in shards:
        steps = jax.random.uniform(jax.random.fold_in(jax.random.fold_in(rng, 6), dim), (blocks,), jnp.float32, low / len(shards), largest / len(shards))
        gain = gain * jnp.repeat(jnp.exp(steps), dims[dim] // blocks).reshape((-1,) + (1,) * (len(dims) - 1 - dim))
    return gain


def scatter_about(stream_key, dims, spread, most, pieces=(), held_as=jnp.bfloat16):
    factor_of = block_scale(stream_key, dims, pieces, -0.22, 0.18) if pieces else 1.0
    drawn = jax.random.normal(stream_key, dims, jnp.float32) * spread * factor_of
    return jnp.minimum(jnp.maximum(drawn, -most), most).astype(held_as)


def setup_inputs(seed: int = 0) -> dict:
    streams_of = jax.random.split(jax.random.key(seed), 4)
    tokens = scatter_about(streams_of[0], (TOKENS, D), 1.0, 6.0, ((0, 4), (1, 8)))
    weight = scatter_about(streams_of[1], (D, FF), D ** -0.5, 0.0625, ((0, 4), (1, 8)))
    out_grad = scatter_about(streams_of[2], (TOKENS, FF), 1.0, 6.0, ((0, 4), (1, 8)))
    return dict(tokens=tokens, weight=weight, out_grad=out_grad)


sqrt_half = 1.0 / math.sqrt(2.0)
inv_root_tau = 1.0 / math.sqrt(2.0 * math.pi)

def gelu_slope(values):
    return 0.5 * (1.0 + jax.scipy.special.erf(values * sqrt_half)) + values * jnp.exp(-0.5 * values * values) * inv_root_tau

def reference(tokens, weight, out_grad):
    full_pre = jnp.dot(tokens, weight, preferred_element_type=jnp.float32)
    preact = full_pre.astype(jnp.bfloat16)
    gradient = (out_grad.astype(jnp.float32) * gelu_slope(full_pre)).astype(jnp.bfloat16)
    input_grad = jnp.dot(gradient, weight.T, preferred_element_type=jnp.float32).astype(jnp.bfloat16)
    return (preact, input_grad)
```

```python
import math

import jax
import jax.numpy as jnp
from jax import lax
from jax.sharding import PartitionSpec as P

sqrt_half = 1.0 / math.sqrt(2.0)
inv_root_tau = 1.0 / math.sqrt(2.0 * math.pi)

CHUNKS = 4


def gelu_slope(values):
    return (
        0.5 * (1.0 + jax.scipy.special.erf(values * sqrt_half))
        + values * jnp.exp(-0.5 * values * values) * inv_root_tau
    )


def pick(blocks, index):
    return lax.dynamic_index_in_dim(blocks, index, 0, keepdims=False)


def gather_tokens(piece, rows, cols):
    mine = lax.all_to_all(piece, "col", 0, 1, tiled=True)
    planes = lax.all_to_all(mine, "row", 1, 0, tiled=True)
    whole = lax.all_gather(planes, "col", axis=0, tiled=False)
    features = whole.shape[-1]
    whole = whole.reshape(cols, rows, -1, features).transpose(1, 0, 2, 3)
    return whole.reshape(-1, features)


def reduce_rows(partial, me, rows):
    far = rows - 1
    right = pick(partial, jnp.minimum(me + far, far))
    left = pick(partial, jnp.maximum(me - far, 0))
    for step in range(far):
        if step:
            right = from_left.astype(jnp.float32) + pick(partial, jnp.minimum(me + far - step, far))
            left = from_right.astype(jnp.float32) + pick(partial, jnp.maximum(me - far + step, 0))
        from_left = lax.ppermute(
            right.astype(jnp.bfloat16), "row", [(j, j + 1) for j in range(far) if j <= step]
        )
        from_right = lax.ppermute(
            left.astype(jnp.bfloat16), "row", [(j, j - 1) for j in range(1, rows) if j >= far - step]
        )
    return pick(partial, me) + from_left.astype(jnp.float32) + from_right.astype(jnp.float32)


def gather_rows(block, rows):
    far = rows - 1
    lefts, rights = [], []
    right = left = block
    for step in range(far):
        right = lax.ppermute(right, "row", [(j, j + 1) for j in range(far) if j >= step])
        left = lax.ppermute(left, "row", [(j, j - 1) for j in range(1, rows) if j <= far - step])
        rights.append(right)
        lefts.append(left)
    return [block] + [lefts[m - 1] + rights[rows - 1 - m] for m in range(1, rows)]


def per_device(rows, cols, tokens, weight, out_grad):
    me = lax.axis_index("row")
    size = out_grad.shape[0] // CHUNKS
    features = weight.shape[0]
    preacts, input_grads = [], []
    for k in range(CHUNKS):
        span = slice(k * size, (k + 1) * size)
        whole = gather_tokens(tokens[span], rows, cols)
        partial = jnp.dot(whole, weight, preferred_element_type=jnp.float32)
        full_pre = reduce_rows(partial.reshape(rows, size, -1), me, rows)
        preacts.append(full_pre.astype(jnp.bfloat16))
        gradient = (out_grad[span].astype(jnp.float32) * gelu_slope(full_pre)).astype(jnp.bfloat16)
        blocks = jnp.concatenate(gather_rows(gradient, rows), axis=0)
        part = lax.dot_general(
            blocks, weight, (((1,), (1,)), ((), ())), preferred_element_type=jnp.float32
        )
        part = part.reshape(rows, cols, size // cols, features).transpose(1, 0, 2, 3)
        owned = lax.psum_scatter(part, "col", scatter_dimension=0, tiled=False)
        owned = jnp.roll(owned, me, axis=0).astype(jnp.bfloat16)
        mine = lax.all_to_all(owned, "row", 0, 2, tiled=True)[0]
        input_grads.append(lax.all_to_all(mine, "col", 1, 0, tiled=True))
    return jnp.concatenate(preacts, axis=0), jnp.concatenate(input_grads, axis=0)


def solution(mesh):
    rows, cols = mesh.shape["row"], mesh.shape["col"]

    def body(tokens, weight, out_grad):
        return per_device(rows, cols, tokens, weight, out_grad)

    return jax.shard_map(
        body,
        mesh=mesh,
        in_specs=(P("row", "col"), P("row", "col"), P("row", "col")),
        out_specs=(P("row", "col"), P("row", "col")),
        check_vma=False,
    )
```

```python
import math

import jax
import jax.numpy as jnp
from jax import lax
from jax.sharding import PartitionSpec as P

sqrt_half = 1.0 / math.sqrt(2.0)
inv_root_tau = 1.0 / math.sqrt(2.0 * math.pi)

CHUNKS = 4
LAG = 1


def gelu_slope(values):
    return (
        0.5 * (1.0 + jax.scipy.special.erf(values * sqrt_half))
        + values * jnp.exp(-0.5 * values * values) * inv_root_tau
    )


def pick(blocks, index):
    return lax.dynamic_index_in_dim(blocks, index, 1, keepdims=False)


class Chunk:
    def __init__(self, partial, out_grad, me, rows):
        self.partial, self.out_grad, self.me, self.rows = partial, out_grad, me, rows
        self.at, self.lefts, self.rights = 0, [], []

    def step(self, *earlier):
        me, rows, far = self.me, self.rows, self.rows - 1
        step = self.at
        self.at += 1
        if step < far:
            right = pick(self.partial, jnp.minimum(me + far - step, far))
            left = pick(self.partial, jnp.maximum(me - far + step, 0))
            if step:
                right = self.right.astype(jnp.float32) + right
                left = self.left.astype(jnp.float32) + left
            right, left = right.astype(jnp.bfloat16), left.astype(jnp.bfloat16)
            reach = [(j, j + 1) for j in range(far) if j <= step]
        else:
            if step == far:
                full_pre = (
                    pick(self.partial, me)
                    + self.right.astype(jnp.float32)
                    + self.left.astype(jnp.float32)
                )
                self.preact = full_pre.astype(jnp.bfloat16)
                self.gradient = (
                    self.out_grad.astype(jnp.float32) * gelu_slope(full_pre)
                ).astype(jnp.bfloat16)
                self.right = self.left = self.gradient
            right, left = self.right, self.left
            reach = [(j, j + 1) for j in range(far) if j >= step - far]
        if earlier:
            right, left = lax.optimization_barrier((right, left) + earlier)[:2]
        self.right = lax.ppermute(right, "row", reach)
        self.left = lax.ppermute(left, "row", [(far - a, far - b) for a, b in reach])
        if step >= far:
            self.rights.append(self.right)
            self.lefts.append(self.left)

    def gathered(self):
        rows = self.rows
        return jnp.stack(
            [self.gradient]
            + [self.lefts[m - 1] + self.rights[rows - 1 - m] for m in range(1, rows)],
            axis=1,
        )


def per_device(rows, cols, tokens, weight, out_grad):
    me = lax.axis_index("row")
    features, hidden = weight.shape
    count = tokens.shape[0] // cols
    size = count // CHUNKS
    mine = lax.all_to_all(tokens, "col", 0, 1, tiled=True)
    planes = lax.all_to_all(mine.reshape(1, count, -1), "row", 2, 0, tiled=True)
    out_grad = out_grad.reshape(cols, CHUNKS, size, hidden)
    steps = 2 * (rows - 1)
    chunks, owned = [], []

    def finish(chunk):
        part = lax.dot_general(
            chunk.gathered().reshape(-1, hidden),
            weight,
            (((1,), (1,)), ((), ())),
            preferred_element_type=jnp.float32,
        ).astype(jnp.bfloat16)
        parts = lax.all_to_all(part.reshape(cols, rows * size, features), "col", 0, 0, tiled=True)
        total = jnp.sum(parts.astype(jnp.float32), axis=0).reshape(rows, size, features)
        owned.append(jnp.roll(total, me, axis=0).astype(jnp.bfloat16))

    whole = [
        lax.all_gather(planes[:, k * size : (k + 1) * size], "col", axis=0, tiled=False)
        for k in range(CHUNKS)
    ]
    for slot in range(2 * (CHUNKS - 1) + steps):
        received = []
        if slot % 2 == 0 and slot // 2 < CHUNKS:
            k = slot // 2
            partial = jnp.dot(
                whole[k].reshape(-1, features), weight, preferred_element_type=jnp.float32
            ).reshape(cols, rows, size, hidden)
            chunks.append(Chunk(partial, out_grad[:, k], me, rows))
        for k, chunk in enumerate(chunks):
            if chunk.at == steps:
                if len(owned) == k and slot >= 2 * k + steps + LAG:
                    finish(chunk)
                    received.append(owned[-1])
                continue
            before = (chunk.right, chunk.left) if chunk.at else ()
            chunk.step(*received)
            received.extend(before)
    for chunk in chunks[len(owned) :]:
        finish(chunk)
    preact = jnp.stack([c.preact.reshape(cols, size, hidden) for c in chunks], axis=1)
    moved = lax.all_to_all(jnp.concatenate(owned, axis=1), "row", 0, 2, tiled=True)[0]
    input_grad = lax.all_to_all(moved, "col", 1, 0, tiled=True)
    return preact.reshape(-1, hidden), input_grad


def solution(mesh):
    rows, cols = mesh.shape["row"], mesh.shape["col"]

    def body(tokens, weight, out_grad):
        return per_device(rows, cols, tokens, weight, out_grad)

    return jax.shard_map(
        body,
        mesh=mesh,
        in_specs=(P("row", "col"), P("row", "col"), P("row", "col")),
        out_specs=(P("row", "col"), P("row", "col")),
        check_vma=False,
    )
```
